512 devices in a mesh: col: 64 (over y, z), row: 8 (over x, core).
Axes of the slice: x: 4, y: 4, z: 16, core: 2. Of those that a mesh axis runs over, the one named last changes fastest.
Arguments:
- x_block: bfloat16 [8, 8192, 64], P('row', 'col'), may hold values from -6 to 6
- tiles: bfloat16 [64, 8, 96, 128, 128], P('col', 'row'), may hold values from -0.078125 to 0.078125
- tile_rows: int32 [64, 8, 96], P('col', 'row'), may hold values from 0 to 63
- tile_cols: int32 [64, 8, 96], P('col', 'row'), may hold values from 0 to 7
- tile_count: int32 [64, 8], P('col', 'row'), may hold values from 1 to 96, as said below
Outputs:
- filtered: bfloat16 [8, 8192, 64], P('row', 'col')
- gram: float32 [64, 64], replicated
The draws below stay inside these ranges and needn't reach their ends.
Inputs may be any that keep to these rules, and one draw needn't show every extreme that they name: `tile_count`: padding slots hold arbitrary tiles and indices; every draw has some device with all 96 slots live.
All inputs are finite; a program needn't handle non-finite values.
Results may differ from the reference program's by a relative error of at most 0.0049.
Values may be sent and summed in bfloat16 or wider, within the bound.
A program may use at most 64 MiB of HBM per device.

```python
import jax
import jax.numpy as jnp
from jax import lax

KV = 64
TILES_DEV = 96
BANDS = 8
SLABS = 64
NB = 512
NDIM = 65536


def draw_tile_count(key, part):
    first_key = jax.random.fold_in(key, 11)
    second_key = jax.random.fold_in(key, 23)
    counts = jax.random.randint(first_key, (SLABS * BANDS,), 1, TILES_DEV + 1)
    chosen = jax.random.randint(second_key, (), 0, SLABS * BANDS)
    counts = jnp.where(jnp.arange(SLABS * BANDS) == chosen, TILES_DEV, counts)
    return counts.reshape(SLABS, BANDS).astype(jnp.int32)


def plant(values, stream_key, least, high):
    spot = [jax.random.randint(jax.random.fold_in(stream_key, axis), (), 0, length) for axis, length in enumerate(values.shape)]
    widest = values.shape.index(max(values.shape))
    next_to = spot[:widest] + [(spot[widest] + 1) % values.shape[widest]] + spot[widest + 1:]
    return values.at[tuple(spot)].set(least).at[tuple(next_to)].set(high)


def level_of(rng, dims, split, least, top_value):
    factor_of, own = 1.0, jax.random.fold_in(rng, 6)
    for axis_at, parts in split:
        draws = jnp.exp(jax.random.uniform(jax.random.fold_in(own, axis_at), (parts,), jnp.float32, least / len(split), top_value / len(split)))
        factor_of = factor_of * jnp.repeat(draws, dims[axis_at] // parts).reshape([-1 if axis == axis_at else 1 for axis in range(len(dims))])
    return factor_of


def bell_draw(key, extent, width, bound, cuts=(), kind=jnp.bfloat16):
    result = jax.random.normal(key, extent, jnp.float32) * width
    if len(cuts) > 0:
        result = level_of(key, extent, cuts, -0.22, 0.18) * result
    return jnp.clip(result, min=-bound, max=bound).astype(kind)


def setup_inputs(seed: int = 0) -> dict:
    arg_keys = jax.random.split(jax.random.key(seed), 6)
    x_block = bell_draw(arg_keys[0], (BANDS, SLABS * 128, KV), 1.0, 6.0, ((0, 8), (1, 64)))
    tiles = bell_draw(arg_keys[1], (SLABS, BANDS, TILES_DEV, 128, 128), (64 * TILES_DEV) ** -0.5, 0.078125, ((0, 64), (1, 8)))
    tile_rows = plant(jax.random.randint(arg_keys[2], (SLABS, BANDS, TILES_DEV), 0, SLABS), jax.random.fold_in(arg_keys[2], 1), 0, SLABS - 1).astype(jnp.int32)
    tile_cols = plant(jax.random.randint(arg_keys[3], (SLABS, BANDS, TILES_DEV), 0, BANDS), jax.random.fold_in(arg_keys[3], 1), 0, BANDS - 1).astype(jnp.int32)
    tile_count = draw_tile_count(jax.random.fold_in(arg_keys[5], 71), 0)
    return dict(x_block=x_block, tiles=tiles, tile_rows=tile_rows, tile_cols=tile_cols, tile_count=tile_count)


def apply_hamiltonian(tiles, tile_rows, tile_cols, tile_count, vec):
    slot_index = jnp.arange(TILES_DEV, dtype=jnp.int32)
    band_index = jnp.arange(BANDS, dtype=jnp.int32)

    def one_slab(acc, items):
        tile_data, rows_here, cols_here, count_here, slab_index = items
        global_cols = cols_here * SLABS + slab_index
        global_rows = band_index[:, None] * SLABS + rows_here
        live = (slot_index[None, :] < count_here[:, None]).astype(jnp.float32)
        picked = vec[global_cols.reshape(-1)].astype(jnp.float32)
        prod = jnp.einsum("tij,tjk->tik", tile_data.reshape(-1, 128, 128).astype(jnp.float32), picked)
        prod = prod * live.reshape(-1)[:, None, None]
        acc = acc + jax.ops.segment_sum(prod, global_rows.reshape(-1), NB)
        return acc, None

    start = jnp.zeros((NB, 128, KV), jnp.float32)
    slabs = jnp.arange(SLABS, dtype=jnp.int32)
    total, _ = lax.scan(one_slab, start, (tiles, tile_rows, tile_cols, tile_count, slabs))
    return total


def reference(x_block, tiles, tile_rows, tile_cols, tile_count):
    vec = x_block.reshape(NB, 128, KV)
    first = apply_hamiltonian(tiles, tile_rows, tile_cols, tile_count, vec).astype(jnp.bfloat16)
    second = apply_hamiltonian(tiles, tile_rows, tile_cols, tile_count, first)
    first_flat = first.reshape(NDIM, KV).astype(jnp.float32)
    second_flat = second.reshape(NDIM, KV)
    gram = jnp.dot(first_flat.T, second_flat, precision=lax.Precision.HIGHEST) / NDIM
    filtered = second.astype(jnp.bfloat16).reshape(BANDS, SLABS * 128, KV)
    return filtered, gram
```

```python
import functools

import jax
import jax.numpy as jnp
from jax import lax
from jax.experimental import pallas as pl
from jax.experimental.pallas import tpu as pltpu
from jax.sharding import PartitionSpec as P

MESH = pl.DeviceIdType.MESH
F32 = jnp.float32
BF16 = jnp.bfloat16
NY, NZ, NROW = 4, 16, 8
SLOTS = 96
CHUNKS = 2
PER = NZ // CHUNKS
HALF = PER // 2
OFFSETS = [8 + ((j + 1) // 2) * (1 if j % 2 == 0 else -1) for j in range(NZ)]
A_SIDE, B_SIDE = 0, 1


def encode(p):
    return (p * jnp.abs(p)).astype(BF16)


def decode(u):
    u = u.astype(F32)
    return u * lax.rsqrt(jnp.maximum(jnp.abs(u), 1e-37))


def rows_to_lanes(a, b):
    i = lax.broadcasted_iota(jnp.int32, (64, 128), 0)
    j = lax.broadcasted_iota(jnp.int32, (64, 128), 1)
    left = jnp.where(i == j, 1.0, 0.0).astype(BF16)
    right = jnp.where(i + 64 == j, 1.0, 0.0).astype(BF16)
    out = jnp.dot(a, left, preferred_element_type=F32)
    return out + jnp.dot(b, right, preferred_element_type=F32)


def kernel(
    table, x_ref, tiles_ref, filtered_ref, gram_ref,
    tile_buf, slab, wide, seg,
    y_far, y_near, y_relay, r_far, r_near, r_relay, z_out, z_in,
    g_send, g_row, g_y, g_z, g_all,
    tile_sem, ag_send, ag_recv, y_send, y_recv, z_send, z_recv, g_ssem, g_rsem,
):
    col, row = lax.axis_index("col"), lax.axis_index("row")
    y, z = lax.div(col, NZ), lax.rem(col, NZ)

    def at_row(step):
        return (col, lax.rem(row + step, NROW))

    def at_y(step):
        return (lax.rem(y + step, NY) * NZ + z, row)

    def at_z(step):
        return (y * NZ + lax.rem(z + step, NZ), row)

    def remote(src, dst, send, recv, device):
        return pltpu.make_async_remote_copy(
            src_ref=src, dst_ref=dst, send_sem=send, recv_sem=recv, device_id=device, device_id_type=MESH
        )

    tile_copy = pltpu.make_async_copy(tiles_ref, tile_buf, tile_sem)
    tile_copy.start()

    barrier = pltpu.get_barrier_semaphore()
    peers = [at_row(i) for i in range(1, NROW)] + [at_y(i) for i in range(1, NY)] + [at_z(i) for i in range(1, NZ)]
    for peer in peers:
        pl.semaphore_signal(barrier, inc=1, device_id=peer, device_id_type=MESH)
    own_x = rows_to_lanes(x_ref[0, 0:64, :], x_ref[0, 64:128, :]).astype(BF16)
    slab[0, row] = own_x
    seg[SLOTS] = jnp.zeros((64, 128), F32)
    pl.semaphore_wait(barrier, len(peers))

    lane = lax.broadcasted_iota(jnp.int32, (64, 128), 1)
    sent = []

    def gather(k):
        for i in range(1, NROW):
            c = remote(slab.at[k, row], slab.at[k, row], ag_send.at[k, i], ag_recv.at[k, i], at_row(i))
            c.start()
            sent.append(c)
        for i in range(1, NROW):
            source = lax.rem(row + NROW - i, NROW)
            remote(
                slab.at[k, source], slab.at[k, source], ag_send.at[k, i], ag_recv.at[k, i], at_row(i)
            ).wait_recv()

    def products(k):
        def widen(r, _):
            here = slab[k, r].astype(F32)
            there = pltpu.roll(here, 64, 1)
            low = lane < 64
            zero = jnp.zeros_like(here)
            wide[r, 0:64, :] = jnp.where(low, here, zero).astype(BF16)
            wide[r, 64:128, :] = jnp.where(low, there, zero).astype(BF16)
            wide[r, 128:192, :] = jnp.where(low, zero, there).astype(BF16)
            wide[r, 192:256, :] = jnp.where(low, zero, here).astype(BF16)
            return 0

        lax.fori_loop(0, NROW, widen, 0)

        group = 8

        def step(i, acc):
            base = i * group
            done = []
            for j in range(group):
                slot = table[0, base + j]
                tile = jnp.concatenate([tile_buf[slot, 0:64, :], tile_buf[slot, 64:128, :]], axis=1)
                done.append(jnp.dot(tile, wide[table[1, base + j]], preferred_element_type=F32))
            for j in range(group):
                acc = acc * table[2, base + j].astype(F32) + done[j]
                seg[base + j] = acc
            return acc

        lax.fori_loop(0, SLOTS // group, step, jnp.zeros((64, 128), F32))

    def partial(y_step, offset):
        block = lax.rem(y + y_step, NY) * NZ + lax.rem(z + offset, NZ)
        return seg[table[3, block]]

    def reduce_scatter(k):
        groups = [[OFFSETS[q * PER + h * HALF : q * PER + (h + 1) * HALF] for h in range(2)] for q in range(CHUNKS)]
        ways = {A_SIDE: (1, NY - 1), B_SIDE: (NY - 1, 1)}
        copies = {}
        for q in range(CHUNKS):
            for h in (A_SIDE, B_SIDE):
                for j, offset in enumerate(groups[q][h]):
                    y_far[k, q, h, j] = encode(partial(2, offset))
                c = remote(
                    y_far.at[k, q, h], r_far.at[k, q, h], y_send.at[k, q, h, 0], y_recv.at[k, q, h, 0], at_y(ways[h][0])
                )
                c.start()
                copies[q, h, 0] = c
        for q in range(CHUNKS):
            for h in (A_SIDE, B_SIDE):
                for j, offset in enumerate(groups[q][h]):
                    y_near[k, q, h, j] = encode(partial(ways[h][1], offset))
                c = remote(
                    y_near.at[k, q, h], r_near.at[k, q, h], y_send.at[k, q, h, 1], y_recv.at[k, q, h, 1], at_y(ways[h][1])
                )
                c.start()
                copies[q, h, 1] = c
            for h in (A_SIDE, B_SIDE):
                copies[q, h, 0].wait_recv()
                for j, offset in enumerate(groups[q][h]):
                    y_relay[k, q, h, j] = encode(partial(ways[h][0], offset) + decode(r_far[k, q, h, j]))
                c = remote(
                    y_relay.at[k, q, h], r_relay.at[k, q, h], y_send.at[k, q, h, 2], y_recv.at[k, q, h, 2], at_y(ways[h][0])
                )
                c.start()
                copies[q, h, 2] = c
        own = None
        for q in range(CHUNKS):
            for h in (A_SIDE, B_SIDE):
                copies[q, h, 1].wait_recv()
                copies[q, h, 2].wait_recv()
                for j, offset in enumerate(groups[q][h]):
                    total = partial(0, offset) + decode(r_near[k, q, h, j]) + decode(r_relay[k, q, h, j])
                    if offset == 0:
                        own = total
                        continue
                    z_out[k, offset] = encode(total)
                    c = remote(
                        z_out.at[k, offset], z_in.at[k, offset], z_send.at[k, offset], z_recv.at[k, offset], at_z(offset)
                    )
                    c.start()
                    copies["z", offset] = c
        for offset in OFFSETS[::-1][1:]:
            copies["z", offset].wait_recv()
            own = own + decode(z_in[k, offset])
        sent.extend(copies.values())
        return own

    gather(0)
    tile_copy.wait()
    products(0)
    first = reduce_scatter(0).astype(BF16)
    slab[1, row] = first
    gather(1)
    products(1)
    second = reduce_scatter(1)

    filtered_ref[0, 0:64, :] = second[:, 0:64].astype(BF16)
    filtered_ref[0, 64:128, :] = pltpu.roll(second, 64, 1)[:, 0:64].astype(BF16)

    turned = first.astype(F32).T.astype(BF16)
    high = second.astype(BF16)
    rest = second - high.astype(F32)
    mid = rest.astype(BF16)
    low = (rest - mid.astype(F32)).astype(BF16)
    both = jnp.dot(turned, low, preferred_element_type=F32)
    both = both + jnp.dot(turned, mid, preferred_element_type=F32)
    both = both + jnp.dot(turned, high, preferred_element_type=F32)
    term = both[0:64, :] + pltpu.roll(both[64:128, :], 64, 1)
    lane32 = lax.broadcasted_iota(jnp.int32, (32, 128), 1)
    packed = jnp.where(lane32 < 64, term[0:32, :], pltpu.roll(term[32:64, :], 64, 1))
    for r in range(NROW):
        g_send[r] = packed[4 * r : 4 * r + 4, :]

    def spread(buf, size, mine, device, sem, source=None):
        for i in range(1, size):
            src = buf.at[mine] if source is None else source(i)
            c = remote(src, buf.at[mine], g_ssem.at[sem + i], g_rsem.at[sem + i], device(i))
            c.start()
            sent.append(c)
        for i in range(1, size):
            other = buf.at[lax.rem(mine + size - i, size)]
            remote(other, other, g_ssem.at[sem + i], g_rsem.at[sem + i], device(i)).wait_recv()

    def added(buf, size):
        total = buf[0]
        for i in range(1, size):
            total = total + buf[i]
        return total

    g_row[row] = g_send[row]
    spread(g_row, NROW, row, at_row, 0, lambda i: g_send.at[lax.rem(row + i, NROW)])
    g_y[y] = added(g_row, NROW)
    spread(g_y, NY, y, at_y, 8)
    g_z[z] = added(g_y, NY)
    spread(g_z, NZ, z, at_z, 16)
    g_all[row] = added(g_z, NZ) * (1.0 / (NROW * NY * NZ * 128))
    spread(g_all, NROW, row, at_row, 32)
    for r in range(NROW):
        piece = g_all[r]
        gram_ref[4 * r : 4 * r + 4, :] = piece[:, 0:64]
        gram_ref[32 + 4 * r : 36 + 4 * r, :] = pltpu.roll(piece, 64, 1)[:, 0:64]
    for c in sent:
        c.wait_send()


def tables(rows, cols, count):
    slot = jnp.arange(SLOTS, dtype=jnp.int32)
    key = jnp.where(slot < count, rows, 64)
    before = (key[None, :] < key[:, None]) | ((key[None, :] == key[:, None]) & (slot[None, :] < slot[:, None]))
    rank = before.astype(jnp.int32).sum(1)
    seen = ((key[None, :] == key[:, None]) & (slot[None, :] < slot[:, None])).any(1).astype(jnp.int32)
    packed = slot + SLOTS * (jnp.clip(cols, 0, NROW - 1) + NROW * seen)
    ordered = jnp.where(rank[None, :] == slot[:, None], packed[None, :], 0).sum(1)
    block = jnp.arange(64, dtype=jnp.int32)
    upto = (key[None, :] <= block[:, None]).astype(jnp.int32).sum(1)
    any_here = (key[None, :] == block[:, None]).any(1)
    last = jnp.where(any_here, upto - 1, SLOTS)
    lines = [ordered % SLOTS, (ordered // SLOTS) % NROW, ordered // (SLOTS * NROW), jnp.pad(last, (0, SLOTS - 64))]
    return jnp.stack(lines).astype(jnp.int32)


def local(x_block, tiles, tile_rows, tile_cols, tile_count):
    table = tables(tile_rows[0, 0], tile_cols[0, 0], tile_count[0, 0])
    dma = pltpu.SemaphoreType.DMA
    vmem = pl.BlockSpec(memory_space=pltpu.VMEM)
    filtered, gram = pl.pallas_call(
        kernel,
        out_shape=(jax.ShapeDtypeStruct((1, 128, 64), BF16), jax.ShapeDtypeStruct((64, 64), F32)),
        in_specs=[pl.BlockSpec(memory_space=pltpu.SMEM), vmem, pl.BlockSpec(memory_space=pl.ANY)],
        out_specs=(vmem, vmem),
        scratch_shapes=[
            pltpu.VMEM((SLOTS, 128, 128), BF16),
            pltpu.VMEM((2, NROW, 64, 128), BF16),
            pltpu.VMEM((NROW, 256, 128), BF16),
            pltpu.VMEM((SLOTS + 1, 64, 128), F32),
            *[pltpu.VMEM((2, CHUNKS, 2, HALF, 64, 128), BF16) for _ in range(6)],
            pltpu.VMEM((2, NZ, 64, 128), BF16),
            pltpu.VMEM((2, NZ, 64, 128), BF16),
            pltpu.VMEM((NROW, 4, 128), F32),
            pltpu.VMEM((NROW, 4, 128), F32),
            pltpu.VMEM((NY, 4, 128), F32),
            pltpu.VMEM((NZ, 4, 128), F32),
            pltpu.VMEM((NROW, 4, 128), F32),
            dma,
            dma((2, NROW)),
            dma((2, NROW)),
            dma((2, CHUNKS, 2, 3)),
            dma((2, CHUNKS, 2, 3)),
            dma((2, NZ)),
            dma((2, NZ)),
            dma((40,)),
            dma((40,)),
        ],
        compiler_params=pltpu.CompilerParams(
            collective_id=0, has_side_effects=True, vmem_limit_bytes=40 * 1024 * 1024
        ),
    )(table, x_block, tiles.reshape(SLOTS, 128, 128))
    return filtered, gram


def solution(mesh):
    placed = (
        P("row", "col", None),
        P("col", "row", None, None, None),
        P("col", "row", None),
        P("col", "row", None),
        P("col", "row"),
    )
    return jax.shard_map(
        local, mesh=mesh, in_specs=placed, out_specs=(P("row", "col", None), P()), check_vma=False
    )
```

```python
import functools

import jax
import jax.numpy as jnp
from jax import lax
from jax.experimental import pallas as pl
from jax.experimental.pallas import tpu as pltpu
from jax.sharding import PartitionSpec as P

MESH = pl.DeviceIdType.MESH
F32 = jnp.float32
BF16 = jnp.bfloat16
NY, NZ, NROW = 4, 16, 8
SLOTS = 96
CHUNKS = 4
PER = NZ // CHUNKS
OFFSETS = [8 + ((j + 1) // 2) * (1 if j % 2 == 0 else -1) for j in range(NZ)]
Y_STEPS = (2, 1, 3)
NT = (((1,), (1,)), ((), ()))


def encode(p):
    return (p * jnp.abs(p)).astype(BF16)


def decode(u):
    u = u.astype(F32)
    return u * lax.rsqrt(jnp.maximum(jnp.abs(u), 1e-37))


def kernel(
    table, x_ref, tiles_ref, filtered_ref, gram_ref,
    tile_buf, slab_x, slab_first, seg, y_out, y_in, z_out, z_in, first_z,
    g_send, g_row, g_y, g_z, g_all,
    in_sem, ag_send, ag_recv, y_send, y_recv, z_send, z_recv, f_send, f_recv, g_ssem, g_rsem,
):
    col, row = lax.axis_index("col"), lax.axis_index("row")
    y, z = lax.div(col, NZ), lax.rem(col, NZ)

    def at_row(step):
        return (col, lax.rem(row + step, NROW))

    def at_y(step):
        return (lax.rem(y + step, NY) * NZ + z, row)

    def at_z(step):
        return (y * NZ + lax.rem(z + step, NZ), row)

    def remote(src, dst, send, recv, device):
        return pltpu.make_async_remote_copy(
            src_ref=src, dst_ref=dst, send_sem=send, recv_sem=recv, device_id=device, device_id_type=MESH
        )

    x_copy = pltpu.make_async_copy(x_ref.at[0], slab_x.at[row], in_sem.at[0])
    x_copy.start()
    tile_copy = pltpu.make_async_copy(tiles_ref, tile_buf, in_sem.at[1])
    tile_copy.start()

    barrier = pltpu.get_barrier_semaphore()
    z_steps = OFFSETS[:-1]
    row_steps = (4, 5, 3, 2, 6, 7, 1)
    peers = [at_z(i) for i in z_steps] + [at_y(i) for i in Y_STEPS] + [at_row(i) for i in row_steps]
    for peer in peers:
        pl.semaphore_signal(barrier, inc=1, device_id=peer, device_id_type=MESH)
    seg[SLOTS] = jnp.zeros((64, 128), F32)
    x_copy.wait()
    pl.semaphore_wait(barrier, len(peers))

    sent = []
    slabs = (slab_x, slab_first)

    def gather_start(k):
        for i in row_steps:
            c = remote(slabs[k].at[row], slabs[k].at[row], ag_send.at[k, i], ag_recv.at[k, i], at_row(i))
            c.start()
            sent.append(c)

    def gather_wait(k):
        for i in row_steps:
            here = slabs[k].at[lax.rem(row + NROW - i, NROW)]
            remote(here, here, ag_send.at[k, i], ag_recv.at[k, i], at_row(i)).wait_recv()

    def products(k):
        group = 8

        def step(i, acc):
            base = i * group
            done = [
                lax.dot_general(
                    slabs[k][table[1, base + j]], tile_buf[table[0, base + j]], NT, preferred_element_type=F32
                )
                for j in range(group)
            ]
            for j in range(group):
                acc = acc * table[2, base + j].astype(F32) + done[j]
                seg[base + j] = acc
            return acc

        lax.fori_loop(0, SLOTS // group, step, jnp.zeros((64, 128), F32))

    def partial(y_step, offset):
        block = lax.rem(y + y_step, NY) * NZ + lax.rem(z + offset, NZ)
        return seg[table[3, block]]

    def scatter_start(k, seen):
        for q in range(CHUNKS):
            offsets = OFFSETS[q * PER : (q + 1) * PER]
            for s in Y_STEPS:
                for j, offset in enumerate(offsets):
                    y_out[k, q, s, j] = encode(partial(s, offset))
                c = remote(y_out.at[k, q, s], y_in.at[k, q, s], y_send.at[k, q, s], y_recv.at[k, q, s], at_y(s))
                c.start()
                sent.append(c)
        own = None
        for q in range(CHUNKS):
            offsets = OFFSETS[q * PER : (q + 1) * PER]
            for s in Y_STEPS:
                remote(
                    y_out.at[k, q, s], y_in.at[k, q, s], y_send.at[k, q, s], y_recv.at[k, q, s], at_y(s)
                ).wait_recv()
            sums = []
            for j, offset in enumerate(offsets):
                total = partial(0, offset)
                for s in Y_STEPS:
                    total = total + decode(y_in[k, q, s, j])
                sums.append(total)
                if offset == 0:
                    own = total
                    continue
                z_out[k, offset] = encode(total)
                c = remote(
                    z_out.at[k, offset], z_in.at[k, offset], z_send.at[k, offset], z_recv.at[k, offset], at_z(offset)
                )
                c.start()
                sent.append(c)
            seen(offsets, sums)
        return own

    def scatter_wait(k, own):
        for offset in z_steps[::-1]:
            here = z_in.at[k, offset]
            remote(z_out.at[k, offset], here, z_send.at[k, offset], z_recv.at[k, offset], at_z(offset)).wait_recv()
            own = own + decode(here[...])
        return own

    gather_start(0)
    tile_copy.wait()
    gather_wait(0)
    products(0)
    first = scatter_wait(0, scatter_start(0, lambda offsets, sums: None)).astype(BF16)
    slab_first[row] = first
    gather_start(1)
    first_z[0] = first
    for i in z_steps:
        c = remote(slab_first.at[row], first_z.at[NZ - i], f_send.at[i], f_recv.at[i], at_z(i))
        c.start()
        sent.append(c)
    gather_wait(1)
    products(1)

    terms = []

    def gram_terms(offsets, sums):
        if not terms:
            for i in z_steps:
                here = first_z.at[NZ - i]
                remote(slab_first.at[row], here, f_send.at[i], f_recv.at[i], at_z(i)).wait_recv()
        left = jnp.concatenate([first_z[offset] for offset in offsets], axis=1)
        right = jnp.concatenate(sums, axis=1)
        high = right.astype(BF16)
        rest = (right - high.astype(F32)).astype(BF16)
        term = lax.dot_general(left, rest, NT, preferred_element_type=F32)
        terms.append(term + lax.dot_general(left, high, NT, preferred_element_type=F32))

    own = scatter_start(1, gram_terms)
    term = terms[0]
    for t in terms[1:]:
        term = term + t
    for r in range(NROW):
        g_send[r] = term[8 * r : 8 * r + 8, :]

    def spread(buf, steps, size, mine, device, sem, source=None):
        for i in steps:
            src = buf.at[mine] if source is None else source(i)
            c = remote(src, buf.at[mine], g_ssem.at[sem + i], g_rsem.at[sem + i], device(i))
            c.start()
            sent.append(c)

        def wait():
            for i in steps:
                other = buf.at[lax.rem(mine + size - i, size)]
                remote(other, other, g_ssem.at[sem + i], g_rsem.at[sem + i], device(i)).wait_recv()

        return wait

    def added(buf, size):
        total = buf[0]
        for i in range(1, size):
            total = total + buf[i]
        return total

    g_row[row] = g_send[row]
    spread(g_row, row_steps, NROW, row, at_row, 0, lambda i: g_send.at[lax.rem(row + i, NROW)])()
    g_y[y] = added(g_row, NROW)
    spread(g_y, Y_STEPS, NY, y, at_y, 8)()
    g_z[z] = added(g_y, NY)
    z_wait = spread(g_z, z_steps, NZ, z, at_z, 16)
    filtered_ref[0] = scatter_wait(1, own).astype(BF16)
    z_wait()
    g_all[row] = added(g_z, NZ) * (1.0 / (NROW * NY * NZ * 128))
    spread(g_all, row_steps, NROW, row, at_row, 32)()
    for r in range(NROW):
        gram_ref[8 * r : 8 * r + 8, :] = g_all[r]
    for c in sent:
        c.wait_send()


def tables(rows, cols, count):
    slot = jnp.arange(SLOTS, dtype=jnp.int32)
    key = jnp.where(slot < count, rows, 64)
    before = (key[None, :] < key[:, None]) | ((key[None, :] == key[:, None]) & (slot[None, :] < slot[:, None]))
    rank = before.astype(jnp.int32).sum(1)
    seen = ((key[None, :] == key[:, None]) & (slot[None, :] < slot[:, None])).any(1).astype(jnp.int32)
    packed = slot + SLOTS * (jnp.clip(cols, 0, NROW - 1) + NROW * seen)
    ordered = jnp.where(rank[None, :] == slot[:, None], packed[None, :], 0).sum(1)
    block = jnp.arange(64, dtype=jnp.int32)
    upto = (key[None, :] <= block[:, None]).astype(jnp.int32).sum(1)
    any_here = (key[None, :] == block[:, None]).any(1)
    last = jnp.where(any_here, upto - 1, SLOTS)
    lines = [ordered % SLOTS, (ordered // SLOTS) % NROW, ordered // (SLOTS * NROW), jnp.pad(last, (0, SLOTS - 64))]
    return jnp.stack(lines).astype(jnp.int32)


def local(x_block, tiles, tile_rows, tile_cols, tile_count):
    table = tables(tile_rows[0, 0], tile_cols[0, 0], tile_count[0, 0])
    dma = pltpu.SemaphoreType.DMA
    vmem = pl.BlockSpec(memory_space=pltpu.VMEM)
    hbm = pl.BlockSpec(memory_space=pl.ANY)
    filtered, gram = pl.pallas_call(
        kernel,
        out_shape=(jax.ShapeDtypeStruct((1, 64, 128), BF16), jax.ShapeDtypeStruct((64, 64), F32)),
        in_specs=[pl.BlockSpec(memory_space=pltpu.SMEM), hbm, hbm],
        out_specs=(vmem, vmem),
        scratch_shapes=[
            pltpu.VMEM((SLOTS, 128, 128), BF16),
            pltpu.VMEM((NROW, 64, 128), BF16),
            pltpu.VMEM((NROW, 64, 128), BF16),
            pltpu.VMEM((SLOTS + 1, 64, 128), F32),
            pltpu.VMEM((2, CHUNKS, NY, PER, 64, 128), BF16),
            pltpu.VMEM((2, CHUNKS, NY, PER, 64, 128), BF16),
            pltpu.VMEM((2, NZ, 64, 128), BF16),
            pltpu.VMEM((2, NZ, 64, 128), BF16),
            pltpu.VMEM((NZ, 64, 128), BF16),
            pltpu.VMEM((NROW, 8, 64), F32),
            pltpu.VMEM((NROW, 8, 64), F32),
            pltpu.VMEM((NY, 8, 64), F32),
            pltpu.VMEM((NZ, 8, 64), F32),
            pltpu.VMEM((NROW, 8, 64), F32),
            dma((2,)),
            dma((2, NROW)),
            dma((2, NROW)),
            dma((2, CHUNKS, NY)),
            dma((2, CHUNKS, NY)),
            dma((2, NZ)),
            dma((2, NZ)),
            dma((NZ,)),
            dma((NZ,)),
            dma((40,)),
            dma((40,)),
        ],
        compiler_params=pltpu.CompilerParams(
            collective_id=0, has_side_effects=True, vmem_limit_bytes=60 * 1024 * 1024
        ),
    )(table, jnp.swapaxes(x_block, 1, 2), tiles.reshape(SLOTS, 128, 128))
    return jnp.swapaxes(filtered, 1, 2), gram


def solution(mesh):
    placed = (
        P("row", "col", None),
        P("col", "row", None, None, None),
        P("col", "row", None),
        P("col", "row", None),
        P("col", "row"),
    )
    return jax.shard_map(
        local, mesh=mesh, in_specs=placed, out_specs=(P("row", "col", None), P()), check_vma=False
    )
```

```python
import functools

import jax
import jax.numpy as jnp
from jax import lax
from jax.experimental import pallas as pl
from jax.experimental.pallas import tpu as pltpu
from jax.sharding import PartitionSpec as P

MESH = pl.DeviceIdType.MESH
F32 = jnp.float32
BF16 = jnp.bfloat16
NY, NZ, NROW = 4, 16, 8
SLOTS = 96
PARTS = 2
WIDE = 64 // PARTS
CHUNKS = 2
PER = NZ // CHUNKS
OFFSETS = [8 + ((j + 1) // 2) * (1 if j % 2 == 0 else -1) for j in range(NZ)]
Y_STEPS = (2, 1, 3)
NT = (((1,), (1,)), ((), ()))


def encode(p):
    return (p * jnp.abs(p)).astype(BF16)


def decode(u):
    u = u.astype(F32)
    return u * lax.rsqrt(jnp.maximum(jnp.abs(u), 1e-37))


def kernel(
    x_ref, tiles_ref, rows_ref, cols_ref, count_ref, filtered_ref, gram_ref,
    tile_buf, rows_buf, cols_buf, lines, table, slab_x0, slab_x1, slab_f0, slab_f1, seg,
    y_out, y_in, z_out, z_in, first_z, g_send, g_row, g_y, g_z, g_all,
    in_sem, ag_send, ag_recv, y_send, y_recv, z_send, z_recv, f_send, f_recv, g_ssem, g_rsem,
):
    col, row = lax.axis_index("col"), lax.axis_index("row")
    y, z = lax.div(col, NZ), lax.rem(col, NZ)

    def at_row(step):
        return (col, lax.rem(row + step, NROW))

    def at_y(step):
        return (lax.rem(y + step, NY) * NZ + z, row)

    def at_z(step):
        return (y * NZ + lax.rem(z + step, NZ), row)

    def remote(src, dst, send, recv, device):
        return pltpu.make_async_remote_copy(
            src_ref=src, dst_ref=dst, send_sem=send, recv_sem=recv, device_id=device, device_id_type=MESH
        )

    slabs = ((slab_x0, slab_x1), (slab_f0, slab_f1))
    inward = [
        pltpu.make_async_copy(rows_ref, rows_buf, in_sem.at[0]),
        pltpu.make_async_copy(cols_ref, cols_buf, in_sem.at[1]),
        *[
            pltpu.make_async_copy(x_ref.at[0, p * WIDE : (p + 1) * WIDE], slabs[0][p].at[row], in_sem.at[3 + p])
            for p in range(PARTS)
        ],
    ]
    for c in inward:
        c.start()
    barrier = pltpu.get_barrier_semaphore()
    z_steps = OFFSETS[:-1]
    row_steps = (4, 5, 3, 2, 6, 7, 1)
    peers = [at_z(i) for i in z_steps] + [at_y(i) for i in Y_STEPS] + [at_row(i) for i in row_steps]
    for peer in peers:
        pl.semaphore_signal(barrier, inc=1, device_id=peer, device_id_type=MESH)
    for p in range(PARTS):
        seg[p, SLOTS] = jnp.zeros((WIDE, 128), F32)
    tile_copy = pltpu.make_async_copy(tiles_ref, tile_buf, in_sem.at[5])
    tile_copy.start()
    for c in inward:
        c.wait()
    lines[...] = tables(rows_buf[...], cols_buf[...], count_ref[0, 0])
    table_copy = pltpu.make_async_copy(lines, table, in_sem.at[6])
    table_copy.start()
    pl.semaphore_wait(barrier, len(peers))

    sent = []

    def waiting(send, recv, ref):
        return remote(ref, ref, send, recv, at_row(1))

    def gather_start(k, p):
        for i in row_steps:
            here = slabs[k][p].at[row]
            remote(here, here, ag_send.at[k, p], ag_recv.at[k, p], at_row(i)).start()
        sent.append(waiting(ag_send.at[k, p], ag_recv.at[k, p], slabs[k][p].at[: NROW - 1]))

    def gather_wait(k, p):
        waiting(ag_send.at[k, p], ag_recv.at[k, p], slabs[k][p].at[: NROW - 1]).wait_recv()

    def products(k, p):
        group = 8

        def step(i, acc):
            base = i * group
            done = [
                lax.dot_general(
                    slabs[k][p][table[1, base + j]], tile_buf[table[0, base + j]], NT, preferred_element_type=F32
                )
                for j in range(group)
            ]
            for j in range(group):
                acc = acc * table[2, base + j].astype(F32) + done[j]
                seg[p, base + j] = acc
            return acc

        lax.fori_loop(0, SLOTS // group, step, jnp.zeros((WIDE, 128), F32))

    def partial(p, y_step, offset):
        block = lax.rem(y + y_step, NY) * NZ + lax.rem(z + offset, NZ)
        return seg[p, table[3, block]]

    def y_start(k, p):
        for q in range(CHUNKS):
            for n, s in enumerate(Y_STEPS):
                for j, offset in enumerate(OFFSETS[q * PER : (q + 1) * PER]):
                    y_out[k, p, q, n, j] = encode(partial(p, s, offset))
                remote(
                    y_out.at[k, p, q, n], y_in.at[k, p, q, n], y_send.at[k, p], y_recv.at[k, p, q], at_y(s)
                ).start()
        sent.append(waiting(y_send.at[k, p], y_recv.at[k, p, 0], y_out.at[k, p]))

    def z_start(k, p, q):
        offsets = OFFSETS[q * PER : (q + 1) * PER]
        waiting(y_send.at[k, p], y_recv.at[k, p, q], y_in.at[k, p, q]).wait_recv()
        sums = []
        for j, offset in enumerate(offsets):
            total = partial(p, 0, offset)
            for n in range(NY - 1):
                total = total + decode(y_in[k, p, q, n, j])
            sums.append(total)
            if offset:
                at = offset - 1
                z_out[k, p, at] = encode(total)
                remote(z_out.at[k, p, at], z_in.at[k, p, at], z_send.at[k, p], z_recv.at[k, p], at_z(offset)).start()
        if q == CHUNKS - 1:
            sent.append(waiting(z_send.at[k, p], z_recv.at[k, p], z_out.at[k, p]))
        return offsets, sums

    def z_wait(k, p, own):
        waiting(z_send.at[k, p], z_recv.at[k, p], z_in.at[k, p]).wait_recv()
        for at in range(NZ - 1):
            own = own + decode(z_in[k, p, at])
        return own

    for p in range(PARTS):
        gather_start(0, p)
    tile_copy.wait()
    table_copy.wait()
    for p in range(PARTS):
        gather_wait(0, p)
        products(0, p)
        y_start(0, p)
    own = []
    for p in range(PARTS):
        for q in range(CHUNKS):
            _, sums = z_start(0, p, q)
        own.append(sums[-1])

    for p in range(PARTS):
        first = z_wait(0, p, own[p]).astype(BF16)
        slabs[1][p][row] = first
        gather_start(1, p)
        first_z[p, 0] = first
        for i in z_steps:
            remote(slabs[1][p].at[row], first_z.at[p, NZ - i], f_send.at[p], f_recv.at[p], at_z(i)).start()
        sent.append(waiting(f_send.at[p], f_recv.at[p], first_z.at[p, 1:]))
    for p in range(PARTS):
        gather_wait(1, p)
        products(1, p)
        y_start(1, p)
    for p in range(PARTS):
        waiting(f_send.at[p], f_recv.at[p], first_z.at[p, 1:]).wait_recv()

    own = []
    for p in range(PARTS):
        term = None
        for q in range(CHUNKS):
            offsets, sums = z_start(1, p, q)
            left = jnp.concatenate(
                [jnp.concatenate([first_z[h, offset] for offset in offsets], axis=1) for h in range(PARTS)], axis=0
            )
            right = jnp.concatenate(sums, axis=1)
            high = right.astype(BF16)
            rest = (right - high.astype(F32)).astype(BF16)
            here = lax.dot_general(rest, left, NT, preferred_element_type=F32)
            here = here + lax.dot_general(high, left, NT, preferred_element_type=F32)
            term = here if term is None else term + here
        own.append(sums[-1])
        for r in range(NROW // PARTS):
            g_send[p * (NROW // PARTS) + r] = term[8 * r : 8 * r + 8, :]

    def spread(buf, steps, size, mine, device, sem, source=None):
        for i in steps:
            src = buf.at[mine] if source is None else source(i)
            remote(src, buf.at[mine], g_ssem.at[sem], g_rsem.at[sem], device(i)).start()
        both = waiting(g_ssem.at[sem], g_rsem.at[sem], buf.at[: size - 1])
        sent.append(both)
        return both.wait_recv

    def added(buf, size):
        total = buf[0]
        for i in range(1, size):
            total = total + buf[i]
        return total

    g_row[row] = g_send[row]
    spread(g_row, row_steps, NROW, row, at_row, 0, lambda i: g_send.at[lax.rem(row + i, NROW)])()
    g_y[y] = added(g_row, NROW)
    spread(g_y, Y_STEPS, NY, y, at_y, 1)()
    g_z[z] = added(g_y, NY)
    g_wait = spread(g_z, z_steps, NZ, z, at_z, 2)
    for p in range(PARTS):
        filtered_ref[0, p * WIDE : (p + 1) * WIDE, :] = z_wait(1, p, own[p]).astype(BF16)
    g_wait()
    g_all[row] = added(g_z, NZ) * (1.0 / (NROW * NY * NZ * 128))
    spread(g_all, row_steps, NROW, row, at_row, 3)()
    gram_ref[...] = jnp.concatenate([g_all[r] for r in range(NROW)], axis=0).T
    for c in sent:
        c.wait_send()


def tables(rows, cols, count):
    size = (SLOTS, SLOTS)
    across = lax.broadcasted_iota(jnp.int32, size, 1)
    down = lax.broadcasted_iota(jnp.int32, size, 0)

    def turned(line):
        return jnp.where(across == down, line, 0).sum(1, keepdims=True)

    key = jnp.where(across[0:1] < count, rows, 64)
    key_down = turned(key)
    equal = (key == key_down) & (across < down)
    rank = jnp.where((key < key_down) | equal, 1, 0).sum(1, keepdims=True)
    seen = jnp.where(equal, 1, 0).max(1, keepdims=True)
    packed = down[:, 0:1] + 128 * (turned(cols & (NROW - 1)) + NROW * seen)
    ordered = jnp.where(rank == across, packed, 0).sum(0, keepdims=True)
    upto = jnp.where(key_down <= across, 1, 0).sum(0, keepdims=True)
    here = jnp.where(key_down == across, 1, 0).sum(0, keepdims=True)
    last = jnp.where(here > 0, upto - 1, SLOTS)
    return jnp.concatenate([ordered & 127, (ordered >> 7) & (NROW - 1), ordered >> 10, last], axis=0)


def local(x_block, tiles, tile_rows, tile_cols, tile_count):
    dma = pltpu.SemaphoreType.DMA
    vmem = pl.BlockSpec(memory_space=pltpu.VMEM)
    filtered, gram = pl.pallas_call(
        kernel,
        out_shape=(jax.ShapeDtypeStruct((1, 64, 128), BF16), jax.ShapeDtypeStruct((64, 64), F32)),
        in_specs=[pl.BlockSpec(memory_space=pltpu.HBM)] * 4 + [pl.BlockSpec(memory_space=pltpu.SMEM)],
        out_specs=(vmem, vmem),
        scratch_shapes=[
            pltpu.VMEM((SLOTS, 128, 128), BF16),
            pltpu.VMEM((1, SLOTS), jnp.int32),
            pltpu.VMEM((1, SLOTS), jnp.int32),
            pltpu.VMEM((4, SLOTS), jnp.int32),
            pltpu.SMEM((4, SLOTS), jnp.int32),
            *[pltpu.VMEM((NROW, WIDE, 128), BF16) for _ in range(2 * PARTS)],
            pltpu.VMEM((PARTS, SLOTS + 1, WIDE, 128), F32),
            pltpu.VMEM((2, PARTS, CHUNKS, NY - 1, PER, WIDE, 128), BF16),
            pltpu.VMEM((2, PARTS, CHUNKS, NY - 1, PER, WIDE, 128), BF16),
            pltpu.VMEM((2, PARTS, NZ - 1, WIDE, 128), BF16),
            pltpu.VMEM((2, PARTS, NZ - 1, WIDE, 128), BF16),
            pltpu.VMEM((PARTS, NZ, WIDE, 128), BF16),
            pltpu.VMEM((NROW, 8, 64), F32),
            pltpu.VMEM((NROW, 8, 64), F32),
            pltpu.VMEM((NY, 8, 64), F32),
            pltpu.VMEM((NZ, 8, 64), F32),
            pltpu.VMEM((NROW, 8, 64), F32),
            dma((7,)),
            *[dma((2, PARTS))] * 3,
            dma((2, PARTS, CHUNKS)),
            *[dma((2, PARTS))] * 2,
            *[dma((PARTS,))] * 2,
            *[dma((4,))] * 2,
        ],
        compiler_params=pltpu.CompilerParams(
            collective_id=0, has_side_effects=True, vmem_limit_bytes=52 * 1024 * 1024
        ),
    )(*[pltpu.with_memory_space_constraint(a, pltpu.HBM) for a in (
        jnp.swapaxes(x_block, 1, 2), tiles.reshape(SLOTS, 128, 128), tile_rows.reshape(1, SLOTS),
        tile_cols.reshape(1, SLOTS),
    )], tile_count)
    return jnp.swapaxes(filtered, 1, 2), gram


def solution(mesh):
    placed = (
        P("row", "col", None),
        P("col", "row", None, None, None),
        P("col", "row", None),
        P("col", "row", None),
        P("col", "row"),
    )
    return jax.shard_map(
        local, mesh=mesh, in_specs=placed, out_specs=(P("row", "col", None), P()), check_vma=False
    )
```

```python
import functools

import jax
import jax.numpy as jnp
from jax import lax
from jax.experimental import pallas as pl
from jax.experimental.pallas import tpu as pltpu
from jax.sharding import PartitionSpec as P

MESH = pl.DeviceIdType.MESH
F32 = jnp.float32
BF16 = jnp.bfloat16
NY, NZ, NROW = 4, 16, 8
SLOTS = 96
PARTS = 2
WIDE = 64 // PARTS
CHUNKS = 4
PER = NZ // CHUNKS
OFFSETS = [8 + ((j + 1) // 2) * (1 if j % 2 == 0 else -1) for j in range(NZ)]
Y_STEPS = (2, 1, 3)
NT = (((1,), (1,)), ((), ()))


def encode(p):
    return (p * jnp.abs(p)).astype(BF16)


def decode(u):
    u = u.astype(F32)
    return u * lax.rsqrt(jnp.maximum(jnp.abs(u), 1e-37))


def kernel(
    x_ref, tiles_ref, rows_ref, cols_ref, count_ref, filtered_ref, gram_ref,
    tile_buf, rows_buf, cols_buf, lines, table, slab_x0, slab_x1, slab_f0, slab_f1, seg,
    y_out, y_in, z_out, z_in, first_z, g_send, g_row, g_y, g_z, g_all,
    in_sem, ag_send, ag_recv, y_send, y_recv, z_send, z_recv, f_send, f_recv, g_ssem, g_rsem,
):
    col, row = lax.axis_index("col"), lax.axis_index("row")
    y, z = lax.div(col, NZ), lax.rem(col, NZ)

    def at_row(step):
        return (col, lax.rem(row + step, NROW))

    def at_y(step):
        return (lax.rem(y + step, NY) * NZ + z, row)

    def at_z(step):
        return (y * NZ + lax.rem(z + step, NZ), row)

    def remote(src, dst, send, recv, device):
        return pltpu.make_async_remote_copy(
            src_ref=src, dst_ref=dst, send_sem=send, recv_sem=recv, device_id=device, device_id_type=MESH
        )

    slabs = ((slab_x0, slab_x1), (slab_f0, slab_f1))
    inward = [
        pltpu.make_async_copy(rows_ref, rows_buf, in_sem.at[0]),
        pltpu.make_async_copy(cols_ref, cols_buf, in_sem.at[1]),
        *[
            pltpu.make_async_copy(x_ref.at[0, p * WIDE : (p + 1) * WIDE], slabs[0][p].at[row], in_sem.at[3 + p])
            for p in range(PARTS)
        ],
    ]
    for c in inward:
        c.start()
    barrier = pltpu.get_barrier_semaphore()
    z_steps = OFFSETS[:-1]
    row_steps = (4, 5, 3, 2, 6, 7, 1)
    peers = [at_z(i) for i in z_steps] + [at_y(i) for i in Y_STEPS] + [at_row(i) for i in row_steps]
    for peer in peers:
        pl.semaphore_signal(barrier, inc=1, device_id=peer, device_id_type=MESH)
    for p in range(PARTS):
        seg[p, SLOTS] = jnp.zeros((WIDE, 128), F32)
    tile_copy = pltpu.make_async_copy(tiles_ref, tile_buf, in_sem.at[5])
    tile_copy.start()
    for c in inward:
        c.wait()
    lines[...] = tables(rows_buf[...], cols_buf[...], count_ref[0, 0])
    table_copy = pltpu.make_async_copy(lines, table, in_sem.at[6])
    table_copy.start()
    pl.semaphore_wait(barrier, len(peers))

    sent = []

    def waiting(send, recv, ref):
        return remote(ref, ref, send, recv, at_row(1))

    def gather_start(k, p):
        for i in row_steps:
            here = slabs[k][p].at[row]
            remote(here, here, ag_send.at[k, p], ag_recv.at[k, p], at_row(i)).start()
        sent.append(waiting(ag_send.at[k, p], ag_recv.at[k, p], slabs[k][p].at[: NROW - 1]))

    def gather_wait(k, p):
        waiting(ag_send.at[k, p], ag_recv.at[k, p], slabs[k][p].at[: NROW - 1]).wait_recv()

    def products(k, p):
        group = 32

        def step(i, acc):
            base = i * group
            done = [
                lax.dot_general(
                    slabs[k][p][table[1, base + j]], tile_buf[table[0, base + j]], NT, preferred_element_type=F32
                )
                for j in range(group)
            ]
            for j in range(group):
                acc = acc * table[2, base + j].astype(F32) + done[j]
                seg[p, base + j] = acc
            return acc

        lax.fori_loop(0, SLOTS // group, step, jnp.zeros((WIDE, 128), F32))

    def partial(p, y_step, offset):
        block = lax.rem(y + y_step, NY) * NZ + lax.rem(z + offset, NZ)
        return seg[p, table[3, block]]

    def y_start(k, p):
        for q in range(CHUNKS):
            for n, s in enumerate(Y_STEPS):
                for j, offset in enumerate(OFFSETS[q * PER : (q + 1) * PER]):
                    y_out[k, p, q, n, j] = encode(partial(p, s, offset))
                remote(
                    y_out.at[k, p, q, n], y_in.at[k, p, q, n], y_send.at[k, p], y_recv.at[k, p, q], at_y(s)
                ).start()
        sent.append(waiting(y_send.at[k, p], y_recv.at[k, p, 0], y_out.at[k, p]))

    def z_start(k, p, q):
        offsets = OFFSETS[q * PER : (q + 1) * PER]
        waiting(y_send.at[k, p], y_recv.at[k, p, q], y_in.at[k, p, q]).wait_recv()
        sums = []
        for j, offset in enumerate(offsets):
            total = partial(p, 0, offset)
            for n in range(NY - 1):
                total = total + decode(y_in[k, p, q, n, j])
            sums.append(total)
            if offset:
                at = offset - 1
                z_out[k, p, at] = encode(total)
                remote(z_out.at[k, p, at], z_in.at[k, p, at], z_send.at[k, p], z_recv.at[k, p], at_z(offset)).start()
        if q == CHUNKS - 1:
            sent.append(waiting(z_send.at[k, p], z_recv.at[k, p], z_out.at[k, p]))
        return offsets, sums

    def z_wait(k, p, own):
        waiting(z_send.at[k, p], z_recv.at[k, p], z_in.at[k, p]).wait_recv()
        for at in range(NZ - 1):
            own = own + decode(z_in[k, p, at])
        return own

    for p in range(PARTS):
        gather_start(0, p)
    tile_copy.wait()
    table_copy.wait()
    for p in range(PARTS):
        gather_wait(0, p)
        products(0, p)
        y_start(0, p)
    own = []
    for p in range(PARTS):
        for q in range(CHUNKS):
            _, sums = z_start(0, p, q)
        own.append(sums[-1])

    for p in range(PARTS):
        first = z_wait(0, p, own[p]).astype(BF16)
        slabs[1][p][row] = first
        gather_start(1, p)
        first_z[p, 0] = first
        for i in z_steps:
            remote(slabs[1][p].at[row], first_z.at[p, NZ - i], f_send.at[p], f_recv.at[p], at_z(i)).start()
        sent.append(waiting(f_send.at[p], f_recv.at[p], first_z.at[p, 1:]))
    for p in range(PARTS):
        gather_wait(1, p)
        products(1, p)
        y_start(1, p)

    own = []
    for p in range(PARTS):
        term = None
        for q in range(CHUNKS):
            offsets, sums = z_start(1, p, q)
            if p == q == 0:
                for h in range(PARTS):
                    waiting(f_send.at[h], f_recv.at[h], first_z.at[h, 1:]).wait_recv()
            left = jnp.concatenate(
                [jnp.concatenate([first_z[h, offset] for offset in offsets], axis=1) for h in range(PARTS)], axis=0
            )
            right = jnp.concatenate(sums, axis=1)
            high = right.astype(BF16)
            rest = (right - high.astype(F32)).astype(BF16)
            here = lax.dot_general(rest, left, NT, preferred_element_type=F32)
            here = here + lax.dot_general(high, left, NT, preferred_element_type=F32)
            term = here if term is None else term + here
        own.append(sums[-1])
        for r in range(NROW // PARTS):
            g_send[p * (NROW // PARTS) + r] = term[8 * r : 8 * r + 8, :]

    def spread(buf, steps, size, mine, device, sem, source=None):
        for i in steps:
            src = buf.at[mine] if source is None else source(i)
            remote(src, buf.at[mine], g_ssem.at[sem], g_rsem.at[sem], device(i)).start()
        both = waiting(g_ssem.at[sem], g_rsem.at[sem], buf.at[: size - 1])
        sent.append(both)
        return both.wait_recv

    def added(buf, size):
        total = buf[0]
        for i in range(1, size):
            total = total + buf[i]
        return total

    g_row[row] = g_send[row]
    spread(g_row, row_steps, NROW, row, at_row, 0, lambda i: g_send.at[lax.rem(row + i, NROW)])()
    g_y[y] = added(g_row, NROW)
    spread(g_y, Y_STEPS, NY, y, at_y, 1)()
    g_z[z] = added(g_y, NY)
    g_wait = spread(g_z, z_steps, NZ, z, at_z, 2)
    for p in range(PARTS):
        filtered_ref[0, p * WIDE : (p + 1) * WIDE, :] = z_wait(1, p, own[p]).astype(BF16)
    g_wait()
    g_all[row] = added(g_z, NZ) * (1.0 / (NROW * NY * NZ * 128))
    spread(g_all, row_steps, NROW, row, at_row, 3)()
    gram_ref[...] = jnp.concatenate([g_all[r] for r in range(NROW)], axis=0).T
    for c in sent:
        c.wait_send()


def tables(rows, cols, count):
    size = (SLOTS, SLOTS)
    across = lax.broadcasted_iota(jnp.int32, size, 1)
    down = lax.broadcasted_iota(jnp.int32, size, 0)

    def turned(line):
        return jnp.where(across == down, line, 0).sum(1, keepdims=True)

    key = jnp.where(across[0:1] < count, rows, 64)
    key_down = turned(key)
    equal = (key == key_down) & (across < down)
    rank = jnp.where((key < key_down) | equal, 1, 0).sum(1, keepdims=True)
    seen = jnp.where(equal, 1, 0).max(1, keepdims=True)
    packed = down[:, 0:1] + 128 * (turned(cols & (NROW - 1)) + NROW * seen)
    ordered = jnp.where(rank == across, packed, 0).sum(0, keepdims=True)
    upto = jnp.where(key_down <= across, 1, 0).sum(0, keepdims=True)
    here = jnp.where(key_down == across, 1, 0).sum(0, keepdims=True)
    last = jnp.where(here > 0, upto - 1, SLOTS)
    return jnp.concatenate([ordered & 127, (ordered >> 7) & (NROW - 1), ordered >> 10, last], axis=0)


def local(x_block, tiles, tile_rows, tile_cols, tile_count):
    dma = pltpu.SemaphoreType.DMA
    vmem = pl.BlockSpec(memory_space=pltpu.VMEM)
    filtered, gram = pl.pallas_call(
        kernel,
        out_shape=(jax.ShapeDtypeStruct((1, 64, 128), BF16), jax.ShapeDtypeStruct((64, 64), F32)),
        in_specs=[pl.BlockSpec(memory_space=pltpu.HBM)] * 4 + [pl.BlockSpec(memory_space=pltpu.SMEM)],
        out_specs=(vmem, vmem),
        scratch_shapes=[
            pltpu.VMEM((SLOTS, 128, 128), BF16),
            pltpu.VMEM((1, SLOTS), jnp.int32),
            pltpu.VMEM((1, SLOTS), jnp.int32),
            pltpu.VMEM((4, SLOTS), jnp.int32),
            pltpu.SMEM((4, SLOTS), jnp.int32),
            *[pltpu.VMEM((NROW, WIDE, 128), BF16) for _ in range(2 * PARTS)],
            pltpu.VMEM((PARTS, SLOTS + 1, WIDE, 128), F32),
            pltpu.VMEM((2, PARTS, CHUNKS, NY - 1, PER, WIDE, 128), BF16),
            pltpu.VMEM((2, PARTS, CHUNKS, NY - 1, PER, WIDE, 128), BF16),
            pltpu.VMEM((2, PARTS, NZ - 1, WIDE, 128), BF16),
            pltpu.VMEM((2, PARTS, NZ - 1, WIDE, 128), BF16),
            pltpu.VMEM((PARTS, NZ, WIDE, 128), BF16),
            pltpu.VMEM((NROW, 8, 64), F32),
            pltpu.VMEM((NROW, 8, 64), F32),
            pltpu.VMEM((NY, 8, 64), F32),
            pltpu.VMEM((NZ, 8, 64), F32),
            pltpu.VMEM((NROW, 8, 64), F32),
            dma((7,)),
            *[dma((2, PARTS))] * 3,
            dma((2, PARTS, CHUNKS)),
            *[dma((2, PARTS))] * 2,
            *[dma((PARTS,))] * 2,
            *[dma((4,))] * 2,
        ],
        compiler_params=pltpu.CompilerParams(
            collective_id=0, has_side_effects=True, vmem_limit_bytes=52 * 1024 * 1024
        ),
    )(*[pltpu.with_memory_space_constraint(a, pltpu.HBM) for a in (
        jnp.swapaxes(x_block, 1, 2), tiles.reshape(SLOTS, 128, 128), tile_rows.reshape(1, SLOTS),
        tile_cols.reshape(1, SLOTS),
    )], tile_count)
    return jnp.swapaxes(filtered, 1, 2), gram


def solution(mesh):
    placed = (
        P("row", "col", None),
        P("col", "row", None, None, None),
        P("col", "row", None),
        P("col", "row", None),
        P("col", "row"),
    )
    return jax.shard_map(
        local, mesh=mesh, in_specs=placed, out_specs=(P("row", "col", None), P()), check_vma=False
    )
```

```python
import functools

import jax
import jax.numpy as jnp
from jax import lax
from jax.experimental import pallas as pl
from jax.experimental.pallas import tpu as pltpu
from jax.sharding import PartitionSpec as P

MESH = pl.DeviceIdType.MESH
F32 = jnp.float32
BF16 = jnp.bfloat16
NY, NZ, NROW = 4, 16, 8
SLOTS = 96
PARTS = 2
WIDE = 64 // PARTS
CHUNKS = 4
PER = NZ // CHUNKS
OFFSETS = [8 + ((j + 1) // 2) * (1 if j % 2 == 0 else -1) for j in range(NZ)]
Y_STEPS = (2, 1, 3)
NT = (((1,), (1,)), ((), ()))


def encode(p):
    return (p * jnp.abs(p)).astype(BF16)


def decode(u):
    u = u.astype(F32)
    return u * lax.rsqrt(jnp.maximum(jnp.abs(u), 1e-37))


def kernel(
    x_ref, tiles_ref, rows_ref, cols_ref, count_ref, filtered_ref, gram_ref,
    tile_buf, rows_buf, cols_buf, lines, table, slab_x0, slab_x1, slab_f0, slab_f1, seg,
    y_out, y_in, z_out, z_in, first_z, g_send, g_plane, g_z, g_all,
    in_sem, ag_send, ag_recv, y_send, y_recv, z_send, z_recv, f_send, f_recv, g_ssem, g_rsem,
):
    col, row = lax.axis_index("col"), lax.axis_index("row")
    y, z = lax.div(col, NZ), lax.rem(col, NZ)

    def at_row(step):
        return (col, lax.rem(row + step, NROW))

    def at_y(step):
        return (lax.rem(y + step, NY) * NZ + z, row)

    def at_z(step):
        return (y * NZ + lax.rem(z + step, NZ), row)

    def remote(src, dst, send, recv, device):
        return pltpu.make_async_remote_copy(
            src_ref=src, dst_ref=dst, send_sem=send, recv_sem=recv, device_id=device, device_id_type=MESH
        )

    slabs = ((slab_x0, slab_x1), (slab_f0, slab_f1))
    inward = [
        pltpu.make_async_copy(rows_ref, rows_buf, in_sem.at[0]),
        pltpu.make_async_copy(cols_ref, cols_buf, in_sem.at[1]),
        *[
            pltpu.make_async_copy(x_ref.at[0, p * WIDE : (p + 1) * WIDE], slabs[0][p].at[row], in_sem.at[3 + p])
            for p in range(PARTS)
        ],
    ]
    for c in inward:
        c.start()
    barrier = pltpu.get_barrier_semaphore()
    z_steps = OFFSETS[:-1]
    row_steps = (4, 5, 3, 2, 6, 7, 1)
    plane_steps = [(s, i) for s in (*Y_STEPS, 0) for i in (*row_steps, 0)][:-1]

    def at_plane(step):
        return (lax.rem(y + step[0], NY) * NZ + z, lax.rem(row + step[1], NROW))

    peers = [at_z(i) for i in z_steps] + [at_plane(step) for step in plane_steps]
    for peer in peers:
        pl.semaphore_signal(barrier, inc=1, device_id=peer, device_id_type=MESH)
    for p in range(PARTS):
        seg[p, SLOTS] = jnp.zeros((WIDE, 128), F32)
    tile_copy = pltpu.make_async_copy(tiles_ref, tile_buf, in_sem.at[5])
    tile_copy.start()
    for c in inward:
        c.wait()
    lines[...] = tables(rows_buf[...], cols_buf[...], count_ref[0, 0])
    table_copy = pltpu.make_async_copy(lines, table, in_sem.at[6])
    table_copy.start()
    pl.semaphore_wait(barrier, len(peers))

    sent = []

    def waiting(send, recv, ref):
        return remote(ref, ref, send, recv, at_row(1))

    def gather_start(k, p):
        for i in row_steps:
            here = slabs[k][p].at[row]
            remote(here, here, ag_send.at[k, p], ag_recv.at[k, p], at_row(i)).start()
        sent.append(waiting(ag_send.at[k, p], ag_recv.at[k, p], slabs[k][p].at[: NROW - 1]))

    def gather_wait(k, p):
        waiting(ag_send.at[k, p], ag_recv.at[k, p], slabs[k][p].at[: NROW - 1]).wait_recv()

    def products(k, p):
        group = 48

        def step(i, acc):
            base = i * group
            done = [
                lax.dot_general(
                    slabs[k][p][table[1, base + j]], tile_buf[table[0, base + j]], NT, preferred_element_type=F32
                )
                for j in range(group)
            ]
            for j in range(group):
                acc = acc * table[2, base + j].astype(F32) + done[j]
                seg[p, base + j] = acc
            return acc

        lax.fori_loop(0, SLOTS // group, step, jnp.zeros((WIDE, 128), F32))

    def partial(p, y_step, offset):
        block = lax.rem(y + y_step, NY) * NZ + lax.rem(z + offset, NZ)
        return seg[p, table[3, block]]

    def y_start(k, p):
        for q in range(CHUNKS):
            for n, s in enumerate(Y_STEPS):
                for j, offset in enumerate(OFFSETS[q * PER : (q + 1) * PER]):
                    y_out[k, p, q, n, j] = encode(partial(p, s, offset))
                remote(
                    y_out.at[k, p, q, n], y_in.at[k, p, q, n], y_send.at[k, p], y_recv.at[k, p, q], at_y(s)
                ).start()
        sent.append(waiting(y_send.at[k, p], y_recv.at[k, p, 0], y_out.at[k, p]))

    def z_start(k, p, q, held=None):
        offsets = OFFSETS[q * PER : (q + 1) * PER]
        waiting(y_send.at[k, p], y_recv.at[k, p, q], y_in.at[k, p, q]).wait_recv()
        sums = []
        for j, offset in enumerate(offsets):
            total = partial(p, 0, offset)
            for n in range(NY - 1):
                total = total + decode(y_in[k, p, q, n, j])
            sums.append(total)
            if offset:
                at = offset - 1
                z_out[k, p, at] = encode(total)
                c = remote(z_out.at[k, p, at], z_in.at[k, p, at], z_send.at[k, p], z_recv.at[k, p], at_z(offset))
                if held is None:
                    c.start()
                else:
                    held.append(c)
        if q == CHUNKS - 1:
            sent.append(waiting(z_send.at[k, p], z_recv.at[k, p], z_out.at[k, p]))
        return offsets, sums

    def z_wait(k, p, own):
        waiting(z_send.at[k, p], z_recv.at[k, p], z_in.at[k, p]).wait_recv()
        for at in range(NZ - 1):
            own = own + decode(z_in[k, p, at])
        return own

    for p in range(PARTS):
        gather_start(0, p)
    tile_copy.wait()
    table_copy.wait()
    for p in range(PARTS):
        gather_wait(0, p)
        products(0, p)
        y_start(0, p)
    own = []
    for p in range(PARTS):
        for q in range(CHUNKS):
            _, sums = z_start(0, p, q)
        own.append(sums[-1])

    def first_over_z(p):
        for i in z_steps:
            remote(slabs[1][p].at[row], first_z.at[p, NZ - i], f_send.at[p], f_recv.at[p], at_z(i)).start()
        sent.append(waiting(f_send.at[p], f_recv.at[p], first_z.at[p, 1:]))

    for p in range(PARTS):
        first = z_wait(0, p, own[p]).astype(BF16)
        slabs[1][p][row] = first
        gather_start(1, p)
        first_z[p, 0] = first
        if p == 0:
            first_over_z(p)
    for p in range(PARTS):
        gather_wait(1, p)
        products(1, p)
        y_start(1, p)
        if p == 0:
            first_over_z(1)

    own, held = [], []
    for p in range(PARTS):
        term = None
        for q in range(CHUNKS):
            offsets, sums = z_start(1, p, q, held if p == PARTS - 1 else None)
            if p == q == 0:
                for h in range(PARTS):
                    waiting(f_send.at[h], f_recv.at[h], first_z.at[h, 1:]).wait_recv()
            left = jnp.concatenate(
                [jnp.concatenate([first_z[h, offset] for offset in offsets], axis=1) for h in range(PARTS)], axis=0
            )
            right = jnp.concatenate(sums, axis=1)
            high = right.astype(BF16)
            rest = (right - high.astype(F32)).astype(BF16)
            here = lax.dot_general(rest, left, NT, preferred_element_type=F32)
            here = here + lax.dot_general(high, left, NT, preferred_element_type=F32)
            term = here if term is None else term + here
        own.append(sums[-1])
        for r in range(NROW // PARTS):
            g_send[p * (NROW // PARTS) + r] = term[8 * r : 8 * r + 8, :]

    def spread(buf, steps, size, mine, device, sem, source=None):
        for i in steps:
            src = buf.at[mine] if source is None else source(i)
            remote(src, buf.at[mine], g_ssem.at[sem], g_rsem.at[sem], device(i)).start()
        both = waiting(g_ssem.at[sem], g_rsem.at[sem], buf.at[: size - 1])
        sent.append(both)
        return both.wait_recv

    def added(buf, size):
        total = buf[0]
        for i in range(1, size):
            total = total + buf[i]
        return total

    mine = y * NROW + row
    g_plane[mine] = g_send[row]
    for step in plane_steps:
        src = g_send.at[lax.rem(row + step[1], NROW)]
        remote(src, g_plane.at[mine], g_ssem.at[0], g_rsem.at[0], at_plane(step)).start()
    plane = waiting(g_ssem.at[0], g_rsem.at[0], g_plane.at[: NY * NROW - 1])
    sent.append(plane)
    for c in held:
        c.start()
    plane.wait_recv()
    g_z[z] = added(g_plane, NY * NROW)
    g_wait = spread(g_z, z_steps, NZ, z, at_z, 2)
    for p in range(PARTS):
        filtered_ref[0, p * WIDE : (p + 1) * WIDE, :] = z_wait(1, p, own[p]).astype(BF16)
    g_wait()
    g_all[row] = added(g_z, NZ) * (1.0 / (NROW * NY * NZ * 128))
    spread(g_all, row_steps, NROW, row, at_row, 3)()
    gram_ref[...] = jnp.concatenate([g_all[r] for r in range(NROW)], axis=0).T
    for c in sent:
        c.wait_send()


def tables(rows, cols, count):
    size = (SLOTS, SLOTS)
    across = lax.broadcasted_iota(jnp.int32, size, 1)
    down = lax.broadcasted_iota(jnp.int32, size, 0)

    def turned(line):
        return jnp.where(across == down, line, 0).sum(1, keepdims=True)

    key = jnp.where(across[0:1] < count, rows, 64)
    key_down = turned(key)
    equal = (key == key_down) & (across < down)
    rank = jnp.where((key < key_down) | equal, 1, 0).sum(1, keepdims=True)
    seen = jnp.where(equal, 1, 0).max(1, keepdims=True)
    packed = down[:, 0:1] + 128 * (turned(cols & (NROW - 1)) + NROW * seen)
    ordered = jnp.where(rank == across, packed, 0).sum(0, keepdims=True)
    upto = jnp.where(key_down <= across, 1, 0).sum(0, keepdims=True)
    here = jnp.where(key_down == across, 1, 0).sum(0, keepdims=True)
    last = jnp.where(here > 0, upto - 1, SLOTS)
    return jnp.concatenate([ordered & 127, (ordered >> 7) & (NROW - 1), ordered >> 10, last], axis=0)


def local(x_block, tiles, tile_rows, tile_cols, tile_count):
    dma = pltpu.SemaphoreType.DMA
    vmem = pl.BlockSpec(memory_space=pltpu.VMEM)
    filtered, gram = pl.pallas_call(
        kernel,
        out_shape=(jax.ShapeDtypeStruct((1, 64, 128), BF16), jax.ShapeDtypeStruct((64, 64), F32)),
        in_specs=[pl.BlockSpec(memory_space=pltpu.HBM)] * 4 + [pl.BlockSpec(memory_space=pltpu.SMEM)],
        out_specs=(vmem, vmem),
        scratch_shapes=[
            pltpu.VMEM((SLOTS, 128, 128), BF16),
            pltpu.VMEM((1, SLOTS), jnp.int32),
            pltpu.VMEM((1, SLOTS), jnp.int32),
            pltpu.VMEM((4, SLOTS), jnp.int32),
            pltpu.SMEM((4, SLOTS), jnp.int32),
            *[pltpu.VMEM((NROW, WIDE, 128), BF16) for _ in range(2 * PARTS)],
            pltpu.VMEM((PARTS, SLOTS + 1, WIDE, 128), F32),
            pltpu.VMEM((2, PARTS, CHUNKS, NY - 1, PER, WIDE, 128), BF16),
            pltpu.VMEM((2, PARTS, CHUNKS, NY - 1, PER, WIDE, 128), BF16),
            pltpu.VMEM((2, PARTS, NZ - 1, WIDE, 128), BF16),
            pltpu.VMEM((2, PARTS, NZ - 1, WIDE, 128), BF16),
            pltpu.VMEM((PARTS, NZ, WIDE, 128), BF16),
            pltpu.VMEM((NROW, 8, 64), F32),
            pltpu.VMEM((NY * NROW, 8, 64), F32),
            pltpu.VMEM((NZ, 8, 64), F32),
            pltpu.VMEM((NROW, 8, 64), F32),
            dma((7,)),
            *[dma((2, PARTS))] * 3,
            dma((2, PARTS, CHUNKS)),
            *[dma((2, PARTS))] * 2,
            *[dma((PARTS,))] * 2,
            *[dma((4,))] * 2,
        ],
        compiler_params=pltpu.CompilerParams(
            collective_id=0, has_side_effects=True, vmem_limit_bytes=52 * 1024 * 1024
        ),
    )(*[pltpu.with_memory_space_constraint(a, pltpu.HBM) for a in (
        jnp.swapaxes(x_block, 1, 2), tiles.reshape(SLOTS, 128, 128), tile_rows.reshape(1, SLOTS),
        tile_cols.reshape(1, SLOTS),
    )], tile_count)
    return jnp.swapaxes(filtered, 1, 2), gram


def solution(mesh):
    placed = (
        P("row", "col", None),
        P("col", "row", None, None, None),
        P("col", "row", None),
        P("col", "row", None),
        P("col", "row"),
    )
    return jax.shard_map(
        local, mesh=mesh, in_specs=placed, out_specs=(P("row", "col", None), P()), check_vma=False
    )
```

```python
import functools

import jax
import jax.numpy as jnp
from jax import lax
from jax.experimental import pallas as pl
from jax.experimental.pallas import tpu as pltpu
from jax.sharding import PartitionSpec as P

MESH = pl.DeviceIdType.MESH
F32 = jnp.float32
BF16 = jnp.bfloat16
NY, NZ, NROW = 4, 16, 8
SLOTS = 96
PARTS = 2
WIDE = 64 // PARTS
CHUNKS = 4
PER = NZ // CHUNKS
OFFSETS = [8 + ((j + 1) // 2) * (1 if j % 2 == 0 else -1) for j in range(NZ)]
Y_STEPS = (2, 1, 3)
NT = (((1,), (1,)), ((), ()))


def encode(p):
    return (p * jnp.abs(p)).astype(BF16)


def decode(u):
    u = u.astype(F32)
    return u * lax.rsqrt(jnp.maximum(jnp.abs(u), 1e-37))


def kernel(
    x_ref, tiles_ref, rows_ref, cols_ref, count_ref, filtered_ref, gram_ref,
    tile_buf, rows_buf, cols_buf, lines, table, slab_x0, slab_x1, slab_f0, slab_f1, seg,
    y_out, y_in, z_out, z_in, first_z, g_send, g_plane, g_z, g_all,
    in_sem, ag_send, ag_recv, y_send, y_recv, z_send, z_recv, f_send, f_recv, g_ssem, g_rsem,
):
    col, row = lax.axis_index("col"), lax.axis_index("row")
    y, z = lax.div(col, NZ), lax.rem(col, NZ)

    def at_row(step):
        return (col, lax.rem(row + step, NROW))

    def at_y(step):
        return (lax.rem(y + step, NY) * NZ + z, row)

    def at_z(step):
        return (y * NZ + lax.rem(z + step, NZ), row)

    def remote(src, dst, send, recv, device):
        return pltpu.make_async_remote_copy(
            src_ref=src, dst_ref=dst, send_sem=send, recv_sem=recv, device_id=device, device_id_type=MESH
        )

    slabs = ((slab_x0, slab_x1), (slab_f0, slab_f1))
    inward = [
        pltpu.make_async_copy(rows_ref, rows_buf, in_sem.at[0]),
        pltpu.make_async_copy(cols_ref, cols_buf, in_sem.at[1]),
        *[
            pltpu.make_async_copy(x_ref.at[0, p * WIDE : (p + 1) * WIDE], slabs[0][p].at[row], in_sem.at[3 + p])
            for p in range(PARTS)
        ],
    ]
    for c in inward:
        c.start()
    barrier = pltpu.get_barrier_semaphore()
    z_steps = OFFSETS[:-1]
    row_steps = (4, 5, 3, 2, 6, 7, 1)
    plane_steps = [(s, i) for s in (*Y_STEPS, 0) for i in (*row_steps, 0)][:-1]

    def at_plane(step):
        return (lax.rem(y + step[0], NY) * NZ + z, lax.rem(row + step[1], NROW))

    peers = [at_z(i) for i in z_steps] + [at_plane(step) for step in plane_steps]
    for peer in peers:
        pl.semaphore_signal(barrier, inc=1, device_id=peer, device_id_type=MESH)
    for p in range(PARTS):
        seg[p, SLOTS] = jnp.zeros((WIDE, 128), F32)
    tile_copy = pltpu.make_async_copy(tiles_ref, tile_buf, in_sem.at[5])
    tile_copy.start()
    for c in inward:
        c.wait()
    lines[...] = tables(rows_buf[...], cols_buf[...], count_ref[0, 0])
    table_copy = pltpu.make_async_copy(lines, table, in_sem.at[6])
    table_copy.start()
    pl.semaphore_wait(barrier, len(peers))

    sent = []

    def waiting(send, recv, ref):
        return remote(ref, ref, send, recv, at_row(1))

    def gather_start(k, p):
        for i in row_steps:
            here = slabs[k][p].at[row]
            remote(here, here, ag_send.at[k, p], ag_recv.at[k, p], at_row(i)).start()
        sent.append(waiting(ag_send.at[k, p], ag_recv.at[k, p], slabs[k][p].at[: NROW - 1]))

    def gather_wait(k, p):
        waiting(ag_send.at[k, p], ag_recv.at[k, p], slabs[k][p].at[: NROW - 1]).wait_recv()

    def products(k, p):
        group = 48

        def step(i, acc):
            base = i * group
            done = [
                lax.dot_general(
                    slabs[k][p][table[1, base + j]], tile_buf[table[0, base + j]], NT, preferred_element_type=F32
                )
                for j in range(group)
            ]
            for j in range(group):
                acc = acc * table[2, base + j].astype(F32) + done[j]
                seg[p, base + j] = acc
            return acc

        lax.fori_loop(0, SLOTS // group, step, jnp.zeros((WIDE, 128), F32))

    def partial(p, y_step, offset):
        block = lax.rem(y + y_step, NY) * NZ + lax.rem(z + offset, NZ)
        return seg[p, table[3, block]]

    def y_start(k, p):
        for q in range(CHUNKS):
            for n, s in enumerate(Y_STEPS):
                for j, offset in enumerate(OFFSETS[q * PER : (q + 1) * PER]):
                    y_out[k, p, q, n, j] = encode(partial(p, s, offset))
                remote(
                    y_out.at[k, p, q, n], y_in.at[k, p, q, n], y_send.at[k, p], y_recv.at[k, p, q], at_y(s)
                ).start()
        sent.append(waiting(y_send.at[k, p], y_recv.at[k, p, 0], y_out.at[k, p]))

    def z_start(k, p, q, held=None):
        offsets = OFFSETS[q * PER : (q + 1) * PER]
        waiting(y_send.at[k, p], y_recv.at[k, p, q], y_in.at[k, p, q]).wait_recv()
        sums = []
        for j, offset in enumerate(offsets):
            total = partial(p, 0, offset)
            for n in range(NY - 1):
                total = total + decode(y_in[k, p, q, n, j])
            sums.append(total)
            if offset:
                at = offset - 1
                z_out[k, p, at] = encode(total)
                c = remote(z_out.at[k, p, at], z_in.at[k, p, at], z_send.at[k, p], z_recv.at[k, p], at_z(offset))
                if held is None:
                    c.start()
                else:
                    held.append(c)
        if q == CHUNKS - 1:
            sent.append(waiting(z_send.at[k, p], z_recv.at[k, p], z_out.at[k, p]))
        return offsets, sums

    def z_wait(k, p, own):
        waiting(z_send.at[k, p], z_recv.at[k, p], z_in.at[k, p]).wait_recv()
        for at in range(NZ - 1):
            own = own + decode(z_in[k, p, at])
        return own

    for p in range(PARTS):
        gather_start(0, p)
    tile_copy.wait()
    table_copy.wait()
    for p in range(PARTS):
        gather_wait(0, p)
        products(0, p)
        y_start(0, p)
    own = []
    for p in range(PARTS):
        for q in range(CHUNKS):
            _, sums = z_start(0, p, q)
        own.append(sums[-1])

    def first_over_z(p):
        for i in z_steps:
            remote(slabs[1][p].at[row], first_z.at[p, NZ - i], f_send.at[p], f_recv.at[p], at_z(i)).start()
        sent.append(waiting(f_send.at[p], f_recv.at[p], first_z.at[p, 1:]))

    for p in range(PARTS):
        first = z_wait(0, p, own[p]).astype(BF16)
        slabs[1][p][row] = first
        gather_start(1, p)
        first_z[p, 0] = first
        if p == 0:
            first_over_z(p)
    for p in range(PARTS):
        gather_wait(1, p)
        products(1, p)
        y_start(1, p)
        if p == 0:
            first_over_z(1)

    mine = y * NROW + row
    shared = NROW // PARTS

    def plane_start(p):
        for s in (*Y_STEPS, 0):
            for j in (2, 1, 3, 0):
                owner = p * shared + lax.rem(row + j, shared)
                c = remote(
                    g_send.at[owner], g_plane.at[mine], g_ssem.at[0], g_rsem.at[0], (lax.rem(y + s, NY) * NZ + z, owner)
                )
                if s or j:
                    c.start()
                else:
                    pl.when(lax.div(row, shared) != p)(c.start)

    own, held = [], []
    for p in range(PARTS):
        term = None
        for q in range(CHUNKS):
            offsets, sums = z_start(1, p, q, held if p == PARTS - 1 else None)
            if p == q == 0:
                for h in range(PARTS):
                    waiting(f_send.at[h], f_recv.at[h], first_z.at[h, 1:]).wait_recv()
            left = jnp.concatenate(
                [jnp.concatenate([first_z[h, offset] for offset in offsets], axis=1) for h in range(PARTS)], axis=0
            )
            right = jnp.concatenate(sums, axis=1)
            high = right.astype(BF16)
            rest = (right - high.astype(F32)).astype(BF16)
            here = lax.dot_general(rest, left, NT, preferred_element_type=F32)
            here = here + lax.dot_general(high, left, NT, preferred_element_type=F32)
            term = here if term is None else term + here
        own.append(sums[-1])
        for r in range(NROW // PARTS):
            g_send[p * (NROW // PARTS) + r] = term[8 * r : 8 * r + 8, :]
        plane_start(p)

    def spread(buf, steps, size, mine, device, sem, source=None):
        for i in steps:
            src = buf.at[mine] if source is None else source(i)
            remote(src, buf.at[mine], g_ssem.at[sem], g_rsem.at[sem], device(i)).start()
        both = waiting(g_ssem.at[sem], g_rsem.at[sem], buf.at[: size - 1])
        sent.append(both)
        return both.wait_recv

    def added(buf, size):
        total = buf[0]
        for i in range(1, size):
            total = total + buf[i]
        return total

    g_plane[mine] = g_send[row]
    plane = waiting(g_ssem.at[0], g_rsem.at[0], g_plane.at[: NY * NROW - 1])
    sent.append(plane)
    for c in held:
        c.start()
    plane.wait_recv()
    g_z[z] = added(g_plane, NY * NROW)
    g_wait = spread(g_z, z_steps, NZ, z, at_z, 2)
    for p in range(PARTS):
        filtered_ref[0, p * WIDE : (p + 1) * WIDE, :] = z_wait(1, p, own[p]).astype(BF16)
    g_wait()
    g_all[row] = added(g_z, NZ) * (1.0 / (NROW * NY * NZ * 128))
    spread(g_all, row_steps, NROW, row, at_row, 3)()
    gram_ref[...] = jnp.concatenate([g_all[r] for r in range(NROW)], axis=0).T
    for c in sent:
        c.wait_send()


def tables(rows, cols, count):
    size = (SLOTS, SLOTS)
    across = lax.broadcasted_iota(jnp.int32, size, 1)
    down = lax.broadcasted_iota(jnp.int32, size, 0)

    def turned(line):
        return jnp.where(across == down, line, 0).sum(1, keepdims=True)

    key = jnp.where(across[0:1] < count, rows, 64)
    key_down = turned(key)
    equal = (key == key_down) & (across < down)
    rank = jnp.where((key < key_down) | equal, 1, 0).sum(1, keepdims=True)
    seen = jnp.where(equal, 1, 0).max(1, keepdims=True)
    packed = down[:, 0:1] + 128 * (turned(cols & (NROW - 1)) + NROW * seen)
    ordered = jnp.where(rank == across, packed, 0).sum(0, keepdims=True)
    upto = jnp.where(key_down <= across, 1, 0).sum(0, keepdims=True)
    here = jnp.where(key_down == across, 1, 0).sum(0, keepdims=True)
    last = jnp.where(here > 0, upto - 1, SLOTS)
    return jnp.concatenate([ordered & 127, (ordered >> 7) & (NROW - 1), ordered >> 10, last], axis=0)


def local(x_block, tiles, tile_rows, tile_cols, tile_count):
    dma = pltpu.SemaphoreType.DMA
    vmem = pl.BlockSpec(memory_space=pltpu.VMEM)
    filtered, gram = pl.pallas_call(
        kernel,
        out_shape=(jax.ShapeDtypeStruct((1, 64, 128), BF16), jax.ShapeDtypeStruct((64, 64), F32)),
        in_specs=[pl.BlockSpec(memory_space=pltpu.HBM)] * 4 + [pl.BlockSpec(memory_space=pltpu.SMEM)],
        out_specs=(vmem, vmem),
        scratch_shapes=[
            pltpu.VMEM((SLOTS, 128, 128), BF16),
            pltpu.VMEM((1, SLOTS), jnp.int32),
            pltpu.VMEM((1, SLOTS), jnp.int32),
            pltpu.VMEM((4, SLOTS), jnp.int32),
            pltpu.SMEM((4, SLOTS), jnp.int32),
            *[pltpu.VMEM((NROW, WIDE, 128), BF16) for _ in range(2 * PARTS)],
            pltpu.VMEM((PARTS, SLOTS + 1, WIDE, 128), F32),
            pltpu.VMEM((2, PARTS, CHUNKS, NY - 1, PER, WIDE, 128), BF16),
            pltpu.VMEM((2, PARTS, CHUNKS, NY - 1, PER, WIDE, 128), BF16),
            pltpu.VMEM((2, PARTS, NZ - 1, WIDE, 128), BF16),
            pltpu.VMEM((2, PARTS, NZ - 1, WIDE, 128), BF16),
            pltpu.VMEM((PARTS, NZ, WIDE, 128), BF16),
            pltpu.VMEM((NROW, 8, 64), F32),
            pltpu.VMEM((NY * NROW, 8, 64), F32),
            pltpu.VMEM((NZ, 8, 64), F32),
            pltpu.VMEM((NROW, 8, 64), F32),
            dma((7,)),
            *[dma((2, PARTS))] * 3,
            dma((2, PARTS, CHUNKS)),
            *[dma((2, PARTS))] * 2,
            *[dma((PARTS,))] * 2,
            *[dma((4,))] * 2,
        ],
        compiler_params=pltpu.CompilerParams(
            collective_id=0, has_side_effects=True, vmem_limit_bytes=52 * 1024 * 1024
        ),
    )(*[pltpu.with_memory_space_constraint(a, pltpu.HBM) for a in (
        jnp.swapaxes(x_block, 1, 2), tiles.reshape(SLOTS, 128, 128), tile_rows.reshape(1, SLOTS),
        tile_cols.reshape(1, SLOTS),
    )], tile_count)
    return jnp.swapaxes(filtered, 1, 2), gram


def solution(mesh):
    placed = (
        P("row", "col", None),
        P("col", "row", None, None, None),
        P("col", "row", None),
        P("col", "row", None),
        P("col", "row"),
    )
    return jax.shard_map(
        local, mesh=mesh, in_specs=placed, out_specs=(P("row", "col", None), P()), check_vma=False
    )
```
